512 devices in a mesh: mem: 8 (over y, z_hi), gx: 64 (over x, z_lo, core).
Axes of the slice: x: 4, y: 4, z: 16 (z_hi: 2, z_lo: 8; z = z_hi * 8 + z_lo), core: 2. Of those that a mesh axis runs over, the one named last changes fastest.
Arguments:
- density: float32 [128, 512, 256], P('mem', 'gx'), may hold values from 0.5 to 2
- momenta: float32 [128, 2, 512, 256], P('mem', None, 'gx'), may hold values from -1 to 1
- desired: float32 [2, 512, 256], P(None, 'gx'), may hold values from -1.5 to 1.5
- factor_x: float32 [512, 128], P('gx'), may hold values from -1 to 1, as said below
- factor_y: float32 [256, 128], replicated, may hold values from -1 to 1, as said below
- factor_m: float32 [128, 32], P('mem'), may hold values from -1 to 1, as said below
Outputs:
- core: float32 [32, 3, 128, 128], P('mem', None, 'gx')
The draws below stay inside these ranges and needn't reach their ends.
Inputs may be any that keep to these rules, and one draw needn't show every extreme that they name: `factor_x`: columns are orthonormal. `factor_y`: columns are orthonormal. `factor_m`: columns are orthonormal.
All inputs are finite; a program needn't handle non-finite values.
Results may differ from the reference program's by a relative error of at most 0.00013.
Values sent between devices are 32-bit elements; how exact they have to be, the bound alone decides.
A program may use at most 64 MiB of HBM per device.

```python
import math
import jax
import jax.numpy as jnp
from jax import lax

MEM_DEV = 16
NY = 256
STEPS = 2
RX = 128
RY = 128
RM = 32
MEMBERS = 128
NX = 512


def draw_factor_x(key, part):
    raw = jax.random.normal(jax.random.fold_in(key, 11), (NX, RX), jnp.float32)
    return jnp.linalg.qr(raw)[0]


def draw_factor_y(key, part):
    raw = jax.random.normal(jax.random.fold_in(key, 12), (NY, RY), jnp.float32)
    return jnp.linalg.qr(raw)[0]


def draw_factor_m(key, part):
    raw = jax.random.normal(jax.random.fold_in(key, 13), (MEMBERS, RM), jnp.float32)
    return jnp.linalg.qr(raw)[0]


def shard_levels(rng, dims, split, low, top_value):
    def one(position, shards_of):
        steps = jax.random.uniform(jax.random.fold_in(jax.random.fold_in(rng, 6), position), (shards_of,), jnp.float32, low / len(split), top_value / len(split))
        return jnp.repeat(jnp.exp(steps), dims[position] // shards_of).reshape((-1,) + (1,) * (len(dims) - position - 1))

    level = one(*split[0])
    for cut in split[1:]:
        level = level * one(*cut)
    return level


def bell_draw(rng, extent, deviation, bound, split=(), dtype=jnp.bfloat16):
    loudness = shard_levels(rng, extent, split, -0.22, 0.18) if split else 1.0
    array = jax.random.normal(rng, extent, jnp.float32) * deviation * loudness
    return jnp.minimum(jnp.maximum(array, -bound), bound).astype(dtype)


def setup_inputs(seed: int = 0) -> dict:
    splits = jax.random.split(jax.random.key(seed), 7)
    density = jnp.clip(0.5 + 1.5 * jax.random.uniform(splits[0], (MEMBERS, NX, NY), jnp.float32) ** shard_levels(splits[0], (MEMBERS, NX, NY), ((0, 8), (1, 64)), -0.2, 0.2), 0.5, 2.0)
    momenta = bell_draw(splits[1], (MEMBERS, 2, NX, NY), 0.3, 1.0, ((0, 8), (2, 64)), jnp.float32)
    desired = bell_draw(splits[2], (2, NX, NY), 0.5, 1.5, ((1, 64),), jnp.float32)
    factor_x = draw_factor_x(jax.random.fold_in(splits[6], 71), 0)
    factor_y = draw_factor_y(jax.random.fold_in(splits[6], 71), 0)
    factor_m = draw_factor_m(jax.random.fold_in(splits[6], 71), 0)
    return dict(density=density, momenta=momenta, desired=desired, factor_x=factor_x, factor_y=factor_y, factor_m=factor_m)


STIFF = 1.0
RELAX = 1.0
DTIME = 0.2

def tendency(fields, desired):
    density = fields[:, 0]
    moment_x = fields[:, 1]
    moment_y = fields[:, 2]
    speed_x = moment_x / density
    speed_y = moment_y / density
    sound = jnp.sqrt(STIFF * density)
    pressure = 0.5 * STIFF * density * density
    conserved = (density, moment_x, moment_y)
    fluxes_x = (moment_x, moment_x * speed_x + pressure, moment_y * speed_x)
    fluxes_y = (moment_y, moment_x * speed_y, moment_y * speed_y + pressure)
    reach_x = jnp.abs(speed_x) + sound
    bound_x = jnp.maximum(reach_x[:, :-1], reach_x[:, 1:])
    reach_y = (jnp.abs(speed_y) + sound)[:, 1:-1]
    bound_y = jnp.maximum(reach_y, jnp.roll(reach_y, -1, axis=-1))
    changes = []
    for quantity, normal_flux, cross_flux in zip(conserved, fluxes_x, fluxes_y):
        face_x = 0.5 * (normal_flux[:, :-1] + normal_flux[:, 1:]) - 0.5 * bound_x * (quantity[:, 1:] - quantity[:, :-1])
        middle = quantity[:, 1:-1]
        cross_mid = cross_flux[:, 1:-1]
        face_y = 0.5 * (cross_mid + jnp.roll(cross_mid, -1, axis=-1)) - 0.5 * bound_y * (jnp.roll(middle, -1, axis=-1) - middle)
        changes.append(-(face_x[:, 1:] - face_x[:, :-1]) - (face_y - jnp.roll(face_y, 1, axis=-1)))
    centre = density[:, 1:-1]
    changes[1] = changes[1] + (centre * desired[0] - moment_x[:, 1:-1]) / RELAX
    changes[2] = changes[2] + (centre * desired[1] - moment_y[:, 1:-1]) / RELAX
    return jnp.stack(changes, axis=1)

def wrap_rows(fields):
    return jnp.concatenate([fields[:, :, -1:], fields, fields[:, :, :1]], axis=2)

def reference(density, momenta, desired, factor_x, factor_y, factor_m):
    block = math.gcd(MEM_DEV, 4)
    count = MEMBERS // block
    dens_blocks = density.reshape(count, block, NX, NY)
    mom_blocks = momenta.reshape(count, block, 2, NX, NY)
    fac_blocks = factor_m.reshape(count, block, RM)
    highest = lax.Precision.HIGHEST

    def advance(carry, inputs):
        dens_part, mom_part, fac_part = inputs
        fields = jnp.concatenate([dens_part[:, None], mom_part], axis=1)
        for repeat in range(STEPS):
            sectioned = fields + DTIME * tendency(wrap_rows(fields), desired)
            second = sectioned + DTIME * tendency(wrap_rows(sectioned), desired)
            fields = 0.5 * fields + 0.5 * second
        along_y = jnp.einsum('mcxy,yb->mcxb', fields, factor_y, precision=highest)
        along_x = jnp.einsum('mcxb,xa->mcab', along_y, factor_x, precision=highest)
        part = jnp.einsum('mcab,mk->kcab', along_x, fac_part, precision=highest)
        return (carry + part, None)
    start = jnp.zeros((RM, 3, RX, RY), jnp.float32)
    core, unused = lax.scan(advance, start, (dens_blocks, mom_blocks, fac_blocks))
    return core
```

```python
import functools

import jax
import jax.numpy as jnp
from jax import lax
from jax.experimental import pallas as pl
from jax.experimental.pallas import tpu as pltpu
from jax.sharding import PartitionSpec as P

Y, ZH, X, ZL, CORES = 4, 2, 4, 8, 2
STEPS = 2
DTIME = 0.2
HALO = 4
MESH = pl.DeviceIdType.MESH
HIGHEST = lax.Precision.HIGHEST


def primitive(q):
    rho, mx, my = q
    inverse = 1.0 / rho
    u = mx * inverse
    v = my * inverse
    sound = jnp.sqrt(rho)
    pressure = 0.5 * rho * rho
    cross = mx * v
    return dict(
        q=q,
        fx=(mx, mx * u + pressure, cross),
        gy=(my, cross, my * v + pressure),
        rx=jnp.abs(u) + sound,
        ry=jnp.abs(v) + sound,
    )


def faces_x(a, b):
    bound = jnp.maximum(a["rx"], b["rx"])
    return tuple(
        (fa + fb) - bound * (qb - qa)
        for fa, fb, qa, qb in zip(a["fx"], b["fx"], a["q"], b["q"])
    )


def ahead(t):
    return pltpu.roll(t, t.shape[-1] - 1, axis=t.ndim - 1)


def behind(t):
    return pltpu.roll(t, 1, axis=t.ndim - 1)


def slopes_y(a):
    bound = jnp.maximum(a["ry"], ahead(a["ry"]))
    q_next = tuple(ahead(t) for t in a["q"])
    g_next = (q_next[2], ahead(a["gy"][1]), ahead(a["gy"][2]))
    out = []
    for g, gn, q, qn in zip(a["gy"], g_next, a["q"], q_next):
        face = (g + gn) - bound * (qn - q)
        out.append(face - behind(face))
    return out


def sweep(source, store, desired_row, low, high, tile):
    def tile_step(index, carry):
        sub = pl.ds(pl.multiple_of(index * tile, tile), tile)

        def row(r):
            return primitive(tuple(source[r, c, sub, :] for c in range(3)))

        before, here = row(low - 1), row(low)
        face_before = faces_x(before, here)
        for r in range(low, high + 1):
            after = row(r + 1)
            face_after = faces_x(here, after)
            gy = slopes_y(here)
            new = []
            for c in range(3):
                flux = (face_after[c] - face_before[c]) + gy[c]
                value = here["q"][c] - (0.5 * DTIME) * flux
                if c:
                    wish = jnp.broadcast_to(desired_row(c - 1, r), value.shape)
                    value = value + DTIME * (here["q"][0] * wish - here["q"][c])
                new.append(value)
            store(r, sub, new)
            here, face_before = after, face_after
        return carry

    return tile_step


def hops(offset, extent):
    return min(offset % extent, (-offset) % extent)


def kernel(
    dens, mom, want, fx, fy, fm, out,
    strip, half, final, want_lo, want_hi, fx_all, weight, turned,
    k_out, k_in, a_out, a_in, b_out, b_in,
    h_send, h_recv, d_send, d_recv, f_send, f_recv,
    k_send, k_recv, a_send, a_recv, b_send, b_recv,
):
    members, rows, ny = dens.shape
    tile = min(members, 8)
    ry = fy.shape[1]
    kb = X
    planes = X * CORES
    nk = Y * ZH * kb
    mem, gx = lax.axis_index("mem"), lax.axis_index("gx")
    y, zh = mem // ZH, mem % ZH
    core = gx % CORES
    zl = (gx // CORES) % ZL
    x = gx // (CORES * ZL)
    xc = x * CORES + core
    z = zh * ZL + zl
    other = (zh + core) % 2

    def device(y_, zh_, x_, zl_, core_):
        return (y_ * ZH + zh_, (x_ * ZL + zl_) * CORES + core_)

    count = X * ZL * CORES
    right = (mem, (gx + 1) % count)
    left = (mem, (gx + count - 1) % count)
    near = [
        (dy, dx, dc)
        for dy in range(Y) for dx in range(X) for dc in range(CORES)
        if dy or dx or dc
    ]
    near.sort(key=lambda o: -(hops(o[0], Y) + hops(o[1], X)))

    def in_plane(dy, dx, dc):
        return (y + dy) % Y, (x + dx) % X, (core + dc) % CORES

    barrier = pltpu.get_barrier_semaphore()

    def greet(who):
        pl.semaphore_signal(barrier, inc=1, device_id=who, device_id_type=MESH)

    greet(right)
    greet(left)
    for i in range(1, ZH * ZL):
        zz = (z + i) % (ZH * ZL)
        greet(device(y, zz // ZL, x, zz % ZL, zh))

    @pl.when(other == 1)
    def _():
        greet(device(y, zh, x, zl, zh))

    for o in near:
        y_, x_, c_ = in_plane(*o)
        greet(device(y_, zh, x_, zl, c_))

    for r in range(rows):
        strip[HALO + r, 0] = dens[:, r, :]
        strip[HALO + r, 1] = mom[:, 0, r, :]
        strip[HALO + r, 2] = mom[:, 1, r, :]

    pl.semaphore_wait(barrier, 2 + (ZH * ZL - 1) + len(near) + other)

    def remote(src, dst, send, recv, who):
        return pltpu.make_async_remote_copy(
            src_ref=src, dst_ref=dst, send_sem=send, recv_sem=recv,
            device_id=who, device_id_type=MESH,
        )

    to_right = remote(
        strip.at[pl.ds(rows, HALO)], strip.at[pl.ds(0, HALO)],
        h_send.at[0], h_recv.at[0], right,
    )
    to_left = remote(
        strip.at[pl.ds(HALO, HALO)], strip.at[pl.ds(HALO + rows, HALO)],
        h_send.at[1], h_recv.at[1], left,
    )
    want_right = remote(want, want_lo, d_send.at[0], d_recv.at[0], right)
    want_left = remote(want, want_hi, d_send.at[1], d_recv.at[1], left)
    halo = [want_right, want_left, to_right, to_left]
    for copy in halo:
        copy.start()

    factor = []
    for o in near:
        if o[0] == 0:
            y_, x_, c_ = in_plane(*o)
            them = x_ * CORES + c_
            copy = remote(
                fx, fx_all.at[xc], f_send.at[them], f_recv.at[xc],
                device(y, zh, x_, zl, c_),
            )
            copy.start()
            factor.append((copy, them))
    fx_all[xc] = fx[...]

    shape = (nk * rows, rows * members)
    pick = (
        lax.broadcasted_iota(jnp.int32, (nk * rows, nk), 0) // rows
        == lax.broadcasted_iota(jnp.int32, (nk * rows, nk), 1)
    ).astype(jnp.float32)
    spread = (
        lax.broadcasted_iota(jnp.int32, (members, rows * members), 1) % members
        == lax.broadcasted_iota(jnp.int32, (members, rows * members), 0)
    ).astype(jnp.float32)
    tall = lax.dot_general(
        pick, fm[...], (((1,), (1,)), ((), ())),
        precision=HIGHEST, preferred_element_type=jnp.float32,
    )
    wide = jnp.dot(tall, spread, precision=HIGHEST, preferred_element_type=jnp.float32)
    same_row = (
        lax.broadcasted_iota(jnp.int32, shape, 0) % rows
        == lax.broadcasted_iota(jnp.int32, shape, 1) // members
    )
    weight[...] = jnp.where(same_row, wide, 0.0)

    for copy, them in factor:
        remote(fx, fx_all.at[them], f_send.at[them], f_recv.at[them], right).wait_recv()
    ranks = fx.shape[1]
    per = ranks // count
    new_a = lax.broadcasted_iota(jnp.int32, (ranks, ranks), 0)
    old_a = lax.broadcasted_iota(jnp.int32, (ranks, ranks), 1)
    t_ = new_a % per
    x_ = (new_a // per) % X
    c_ = (new_a // (per * X)) % CORES
    zl_ = new_a // (per * X * CORES)
    order = (old_a == ((x_ * ZL + zl_) * CORES + c_) * per + t_).astype(jnp.float32)
    turned[...] = lax.dot_general(
        order, fx_all[...].reshape(planes * rows, ranks), (((1,), (1,)), ((), ())),
        precision=HIGHEST, preferred_element_type=jnp.float32,
    )

    def desired_row(c, r):
        if r < HALO:
            return want_lo[c, pl.ds(rows - HALO + r, 1), :]
        if r < HALO + rows:
            return want[c, pl.ds(r - HALO, 1), :]
        return want_hi[c, pl.ds(r - HALO - rows, 1), :]

    for copy in halo:
        copy.wait_recv()
    for copy in halo:
        copy.wait_send()

    low, high = 1, rows + 2 * HALO - 2
    for step in range(STEPS):
        def keep(r, sub, new):
            for c in range(3):
                half[r, c, sub, :] = new[c]

        lax.fori_loop(
            0, members // tile, sweep(strip, keep, desired_row, low, high, tile), 0
        )
        low, high = low + 1, high - 1
        last = step == STEPS - 1

        def blend(r, sub, new):
            for c in range(3):
                value = 0.5 * strip[r, c, sub, :] + 0.5 * new[c]
                if last:
                    final[c, r - HALO, sub, :] = value
                else:
                    strip[r, c, sub, :] = value

        lax.fori_loop(
            0, members // tile, sweep(half, blend, desired_row, low, high, tile), 0
        )
        low, high = low + 1, high - 1

    along_y = jnp.dot(
        final[...].reshape(3 * rows * members, ny), fy[...],
        precision=HIGHEST, preferred_element_type=jnp.float32,
    ).reshape(3, rows * members, ry)
    for c in range(3):
        k_out[:, c] = jnp.dot(
            weight[...], along_y[c], precision=HIGHEST, preferred_element_type=jnp.float32
        ).reshape(nk, rows, ry)

    def k_of(y_, x_, c_):
        return (y_ * ZH + c_) * kb + x_

    k_copies = []
    for o in near:
        y_, x_, c_ = in_plane(*o)
        slot = y_ * planes + x_ * CORES + c_
        copy = remote(
            k_out.at[k_of(y_, x_, c_)], k_in.at[y * planes + xc],
            k_send.at[slot], k_recv.at[y * planes + xc], device(y_, zh, x_, zl, c_),
        )
        copy.start()
        k_copies.append((copy, slot))
    k_in[y * planes + xc] = k_out[k_of(y, x, core)]
    for copy, slot in reversed(k_copies):
        remote(
            k_out.at[0], k_in.at[slot], k_send.at[slot], k_recv.at[slot], right
        ).wait_recv()
    total = k_in[pl.ds(0, planes)]
    for i in range(1, Y):
        total = total + k_in[pl.ds(i * planes, planes)]

    for c in range(3):
        a_out[:, c] = jnp.dot(
            turned[...], total[:, c].reshape(planes * rows, ry),
            precision=HIGHEST, preferred_element_type=jnp.float32,
        ).reshape(ZL * CORES, per * X, ry)

    a_copies = []
    far = sorted(range(ZL), key=lambda s: (hops(s, ZL) * -1, s))
    for i in range(ZL):
        s = far[i] + other * (far[ZL - 1 - i] - far[i])
        zl_t = (zl + s) % ZL
        for d in (1, 0):
            c_t = (core + d) % CORES
            slot = zl_t * CORES + c_t
            copy = remote(
                a_out.at[slot], a_in.at[z], a_send.at[slot], a_recv.at[z],
                device(y, core, x, zl_t, c_t),
            )
            if i == ZL - 1 and d == 0:
                @pl.when(other == 1)
                def _():
                    copy.start()

                @pl.when(other == 0)
                def _():
                    a_in[z] = a_out[zl * CORES + core]
            else:
                copy.start()
                a_copies.append(copy)
            last_copy = copy

    def landed(slot):
        remote(
            a_out.at[0], a_in.at[slot], a_send.at[0], a_recv.at[slot], right
        ).wait_recv()

    @pl.when(other == 1)
    def _():
        landed(z)

    for i in range(1, ZH * ZL):
        landed((z + i) % (ZH * ZL))
    piece = a_in[0]
    for i in range(1, ZH * ZL):
        piece = piece + a_in[i]

    for i in range(X):
        b_out[i] = piece[:, i * per:(i + 1) * per, :]
    b_copies = []
    for dx in (2, 1, 3) if X == 4 else range(1, X):
        x_t = (x + dx) % X
        copy = remote(
            b_out.at[x_t], b_in.at[x], b_send.at[x_t], b_recv.at[x],
            device(y, zh, x_t, zl, core),
        )
        copy.start()
        b_copies.append((copy, x_t))
    b_in[x] = b_out[x]
    for copy, x_t in b_copies:
        remote(b_out.at[0], b_in.at[x_t], b_send.at[x_t], b_recv.at[x_t], right).wait_recv()
    out[...] = b_in[...]

    for copy, _slot in factor + k_copies + b_copies:
        copy.wait_send()
    for copy in a_copies:
        copy.wait_send()

    @pl.when(other == 1)
    def _():
        last_copy.wait_send()


def on_device(density, momenta, desired, factor_x, factor_y, factor_m):
    members, rows, ny = density.shape
    ranks = factor_x.shape[1]
    ry = factor_y.shape[1]
    count = X * ZL * CORES
    per = ranks // count
    planes = X * CORES
    nk = Y * ZH * X
    f32 = jnp.float32
    vmem = pl.BlockSpec(memory_space=pltpu.VMEM)
    dma = pltpu.SemaphoreType.DMA
    strip = (rows + 2 * HALO, 3, members, ny)
    return pl.pallas_call(
        kernel,
        out_shape=jax.ShapeDtypeStruct((X, 3, per, ry), f32),
        in_specs=[vmem] * 6,
        out_specs=vmem,
        scratch_shapes=[
            pltpu.VMEM(strip, f32),
            pltpu.VMEM(strip, f32),
            pltpu.VMEM((3, rows, members, ny), f32),
            pltpu.VMEM((2, rows, ny), f32),
            pltpu.VMEM((2, rows, ny), f32),
            pltpu.VMEM((planes, rows, ranks), f32),
            pltpu.VMEM((nk * rows, rows * members), f32),
            pltpu.VMEM((ranks, planes * rows), f32),
            pltpu.VMEM((nk, 3, rows, ry), f32),
            pltpu.VMEM((Y * planes, 3, rows, ry), f32),
            pltpu.VMEM((ZL * CORES, 3, per * X, ry), f32),
            pltpu.VMEM((ZH * ZL, 3, per * X, ry), f32),
            pltpu.VMEM((X, 3, per, ry), f32),
            pltpu.VMEM((X, 3, per, ry), f32),
            dma((2,)), dma((2,)), dma((2,)), dma((2,)),
            dma((planes,)), dma((planes,)),
            dma((Y * planes,)), dma((Y * planes,)),
            dma((ZL * CORES,)), dma((ZH * ZL,)),
            dma((X,)), dma((X,)),
        ],
        compiler_params=pltpu.CompilerParams(
            collective_id=0, has_side_effects=True, vmem_limit_bytes=48 * 1024 * 1024
        ),
    )(density, momenta, desired, factor_x, factor_y, factor_m)


def solution(mesh):
    return jax.shard_map(
        on_device,
        mesh=mesh,
        in_specs=(
            P("mem", "gx", None),
            P("mem", None, "gx", None),
            P(None, "gx", None),
            P("gx", None),
            P(),
            P("mem", None),
        ),
        out_specs=P("mem", None, "gx", None),
        check_vma=False,
    )
```

```python
import functools

import jax
import jax.numpy as jnp
from jax import lax
from jax.experimental import pallas as pl
from jax.experimental.pallas import tpu as pltpu
from jax.sharding import PartitionSpec as P

Y, ZH, X, ZL, CORES = 4, 2, 4, 8, 2
STEPS = 2
DTIME = 0.2
HALO = 4
MESH = pl.DeviceIdType.MESH
HIGHEST = lax.Precision.HIGHEST


def primitive(q):
    rho, mx, my = q
    inverse = 1.0 / rho
    u = mx * inverse
    v = my * inverse
    sound = jnp.sqrt(rho)
    pressure = 0.5 * rho * rho
    cross = mx * v
    return dict(
        q=q,
        fx=(mx, mx * u + pressure, cross),
        gy=(my, cross, my * v + pressure),
        rx=jnp.abs(u) + sound,
        ry=jnp.abs(v) + sound,
    )


def faces_x(a, b):
    bound = jnp.maximum(a["rx"], b["rx"])
    return tuple(
        (fa + fb) - bound * (qb - qa)
        for fa, fb, qa, qb in zip(a["fx"], b["fx"], a["q"], b["q"])
    )


def ahead(t):
    return pltpu.roll(t, t.shape[-1] - 1, axis=t.ndim - 1)


def behind(t):
    return pltpu.roll(t, 1, axis=t.ndim - 1)


def slopes_y(a):
    bound = jnp.maximum(a["ry"], ahead(a["ry"]))
    q_next = tuple(ahead(t) for t in a["q"])
    g_next = (q_next[2], ahead(a["gy"][1]), ahead(a["gy"][2]))
    out = []
    for g, gn, q, qn in zip(a["gy"], g_next, a["q"], q_next):
        face = (g + gn) - bound * (qn - q)
        out.append(face - behind(face))
    return out


def sweep(source, store, desired_row, start, count, tile):
    def tile_step(index, carry):
        sub = pl.ds(pl.multiple_of(index * tile, tile), tile)

        def row(r):
            return primitive(tuple(source[r, c, sub, :] for c in range(3)))

        before, here = row(start - 1), row(start)
        face_before = faces_x(before, here)
        for i in range(count):
            r = start + i
            after = row(r + 1)
            face_after = faces_x(here, after)
            gy = slopes_y(here)
            new = []
            for c in range(3):
                flux = (face_after[c] - face_before[c]) + gy[c]
                value = here["q"][c] - (0.5 * DTIME) * flux
                if c:
                    wish = jnp.broadcast_to(desired_row(c - 1, r), value.shape)
                    value = value + DTIME * (here["q"][0] * wish - here["q"][c])
                new.append(value)
            store(r, sub, new)
            here, face_before = after, face_after
        return carry

    return tile_step


def hops(offset, extent):
    return min(offset % extent, (-offset) % extent)


def kernel(
    dens_hbm, mom_hbm, want_hbm, fx_hbm, fy_hbm, fm_hbm, out,
    dens, mom, want, fx_all, fy, fm,
    strip0, strip1, strip2, strip3, final, weight, turned, gathered,
    k_out, k_in, a_out, a_in, b_out, b_in,
    in_sem, h_send, h_recv, d_send, d_recv, f_send, f_recv,
    k_send, k_recv, a_send, a_recv, b_send, b_recv,
):
    members, rows, ny = dens_hbm.shape
    tile = min(members, 8)
    ry = fy.shape[1]
    kb = X
    planes = X * CORES
    nk = Y * ZH * kb
    mem, gx = lax.axis_index("mem"), lax.axis_index("gx")
    y, zh = mem // ZH, mem % ZH
    core = gx % CORES
    zl = (gx // CORES) % ZL
    x = gx // (CORES * ZL)
    xc = x * CORES + core
    z = zh * ZL + zl
    other = (zh + core) % 2

    def device(y_, zh_, x_, zl_, core_):
        return (y_ * ZH + zh_, (x_ * ZL + zl_) * CORES + core_)

    count = X * ZL * CORES
    right = (mem, (gx + 1) % count)
    left = (mem, (gx + count - 1) % count)
    near = [
        (dy, dx, dc)
        for dy in range(Y) for dx in range(X) for dc in range(CORES)
        if dy or dx or dc
    ]
    near.sort(key=lambda o: -(hops(o[0], Y) + hops(o[1], X)))

    def in_plane(dy, dx, dc):
        return (y + dy) % Y, (x + dx) % X, (core + dc) % CORES

    fetch = [
        pltpu.make_async_copy(src, dst, in_sem.at[i])
        for i, (src, dst) in enumerate([
            (dens_hbm, dens), (mom_hbm, mom), (want_hbm, want.at[:, pl.ds(rows, rows), :]),
            (fx_hbm, fx_all.at[xc]), (fy_hbm, fy), (fm_hbm, fm),
        ])
    ]
    for copy in fetch:
        copy.start()

    barrier = pltpu.get_barrier_semaphore()

    def greet(who):
        pl.semaphore_signal(barrier, inc=1, device_id=who, device_id_type=MESH)

    greet(right)
    greet(left)
    for i in range(1, ZH * ZL):
        zz = (z + i) % (ZH * ZL)
        greet(device(y, zz // ZL, x, zz % ZL, zh))

    @pl.when(other == 1)
    def _():
        greet(device(y, zh, x, zl, zh))

    for o in near:
        y_, x_, c_ = in_plane(*o)
        greet(device(y_, zh, x_, zl, c_))

    for copy in fetch[:2]:
        copy.wait()
    for r in range(rows):
        strip0[HALO + r, 0] = dens[:, r, :]
        strip0[HALO + r, 1] = mom[:, 0, r, :]
        strip0[HALO + r, 2] = mom[:, 1, r, :]

    pl.semaphore_wait(barrier, 2 + (ZH * ZL - 1) + len(near) + other)

    def remote(src, dst, send, recv, who):
        return pltpu.make_async_remote_copy(
            src_ref=src, dst_ref=dst, send_sem=send, recv_sem=recv,
            device_id=who, device_id_type=MESH,
        )

    to_right = remote(
        strip0.at[pl.ds(rows, HALO)], strip0.at[pl.ds(0, HALO)],
        h_send.at[0], h_recv.at[0], right,
    )
    to_left = remote(
        strip0.at[pl.ds(HALO, HALO)], strip0.at[pl.ds(HALO + rows, HALO)],
        h_send.at[1], h_recv.at[1], left,
    )
    want_right = remote(
        want_hbm, want.at[:, pl.ds(0, rows), :], d_send.at[0], d_recv.at[0], right
    )
    want_left = remote(
        want_hbm, want.at[:, pl.ds(2 * rows, rows), :], d_send.at[1], d_recv.at[1], left
    )
    later_right = (core == 1) & (zl <= 2)
    later_left = (core == 0) & (zl >= ZL - 3)

    @pl.when(jnp.logical_not(later_right))
    def _():
        to_right.start()

    @pl.when(jnp.logical_not(later_left))
    def _():
        to_left.start()

    want_right.start()
    want_left.start()

    factor = []
    for o in near:
        if o[0] == 0:
            y_, x_, c_ = in_plane(*o)
            them = x_ * CORES + c_
            copy = remote(
                fx_hbm, fx_all.at[xc], f_send.at[them], f_recv.at[xc],
                device(y, zh, x_, zl, c_),
            )
            copy.start()
            factor.append((copy, them))
    for copy in fetch[2:]:
        copy.wait()

    def desired_row(c, r):
        return want[c, pl.ds(r + rows - HALO, 1), :]

    strips = (strip0, strip1, strip2, strip3)

    def section(e, start, count, side=None):
        def store(r, sub, new):
            for c in range(3):
                value = new[c]
                if e % 2:
                    value = 0.5 * strips[e - 1][r, c, sub, :] + 0.5 * value
                if e == 2 * STEPS - 1:
                    final[c, r - start, sub, :] = value
                else:
                    strips[e + 1][r, c, sub, :] = value

        lax.fori_loop(
            0, members // tile, sweep(strips[e], store, desired_row, start, count, tile), 0
        )

    for e in range(2 * STEPS - 1):
        section(e, HALO + 1 + e, rows - 2 - 2 * e)

    shape = (nk * rows, HALO * members)
    pick = (
        lax.broadcasted_iota(jnp.int32, (nk * rows, nk), 0) // rows
        == lax.broadcasted_iota(jnp.int32, (nk * rows, nk), 1)
    ).astype(jnp.float32)
    spread = (
        lax.broadcasted_iota(jnp.int32, (members, HALO * members), 1) % members
        == lax.broadcasted_iota(jnp.int32, (members, HALO * members), 0)
    ).astype(jnp.float32)
    tall = lax.dot_general(
        pick, fm[...], (((1,), (1,)), ((), ())),
        precision=HIGHEST, preferred_element_type=jnp.float32,
    )
    wide = jnp.dot(tall, spread, precision=HIGHEST, preferred_element_type=jnp.float32)
    same_row = (
        lax.broadcasted_iota(jnp.int32, shape, 0) % rows
        == lax.broadcasted_iota(jnp.int32, shape, 1) // members
    )
    weight[...] = jnp.where(same_row, wide, 0.0)

    @pl.when(later_right)
    def _():
        to_right.start()

    @pl.when(later_left)
    def _():
        to_left.start()

    for copy, them in factor:
        remote(fx_hbm, fx_all.at[them], f_send.at[them], f_recv.at[them], right).wait_recv()
    ranks = fx_all.shape[2]
    per = ranks // count
    new_a = lax.broadcasted_iota(jnp.int32, (ranks, ranks), 0)
    old_a = lax.broadcasted_iota(jnp.int32, (ranks, ranks), 1)
    t_ = new_a % per
    x_ = (new_a // per) % X
    c_ = (new_a // (per * X)) % CORES
    zl_ = new_a // (per * X * CORES)
    order = (old_a == ((x_ * ZL + zl_) * CORES + c_) * per + t_).astype(jnp.float32)
    turned[...] = lax.dot_general(
        order, fx_all[...].reshape(planes * rows, ranks), (((1,), (1,)), ((), ())),
        precision=HIGHEST, preferred_element_type=jnp.float32,
    )

    def k_of(y_, x_, c_):
        return (y_ * ZH + c_) * kb + x_

    mine = y * planes + xc

    def k_copy(side, o):
        y_, x_, c_ = in_plane(*o)
        slot = y_ * planes + x_ * CORES + c_
        return remote(
            k_out.at[side, k_of(y_, x_, c_)], k_in.at[side, mine],
            k_send.at[side, slot], k_recv.at[side, mine], device(y_, zh, x_, zl, c_),
        )

    def one_side(turn, carry):
        side = (1 - core) + turn * (2 * core - 1)
        remote(
            strip0.at[pl.ds(HALO, HALO)], strip0.at[pl.ds(side * (HALO + rows), HALO)],
            h_send.at[side], h_recv.at[side], right,
        ).wait_recv()
        remote(
            want_hbm, want.at[:, pl.ds(pl.multiple_of(side * 2 * rows, rows), rows), :],
            d_send.at[side], d_recv.at[side], right,
        ).wait_recv()
        for e in range(2 * STEPS):
            section(e, 1 + e + side * (rows + 2 - 2 * e), HALO)
        along_y = jnp.dot(
            final[...].reshape(3 * HALO * members, ny), fy[...],
            precision=HIGHEST, preferred_element_type=jnp.float32,
        ).reshape(3, HALO * members, ry)
        for c in range(3):
            k_out[side, :, c] = jnp.dot(
                weight[...], along_y[c], precision=HIGHEST, preferred_element_type=jnp.float32
            ).reshape(nk, rows, ry)[:, :HALO]
        for o in near:
            k_copy(side, o).start()
        k_in[side, mine] = k_out[side, k_of(y, x, core)]
        return carry

    lax.fori_loop(0, 2, one_side, 0)

    for side in range(2):
        for o in reversed(near):
            y_, x_, c_ = in_plane(*o)
            slot = y_ * planes + x_ * CORES + c_
            remote(
                k_out.at[0, 0], k_in.at[side, slot],
                k_send.at[side, slot], k_recv.at[side, slot], right,
            ).wait_recv()
    for side in range(2):
        total = k_in[side, pl.ds(0, planes)]
        for i in range(1, Y):
            total = total + k_in[side, pl.ds(i * planes, planes)]
        for c in range(3):
            for i in range(planes):
                gathered[c, pl.ds(i * rows + side * HALO, HALO), :] = total[i, c]

    for c in range(3):
        a_out[:, c] = jnp.dot(
            turned[...], gathered[c],
            precision=HIGHEST, preferred_element_type=jnp.float32,
        ).reshape(ZL * CORES, per * X, ry)

    a_copies = []
    far = sorted(range(ZL), key=lambda s: (hops(s, ZL) * -1, s))
    for i in range(ZL):
        s = far[i] + other * (far[ZL - 1 - i] - far[i])
        zl_t = (zl + s) % ZL
        for d in (1, 0):
            c_t = (core + d) % CORES
            slot = zl_t * CORES + c_t
            copy = remote(
                a_out.at[slot], a_in.at[z], a_send.at[slot], a_recv.at[z],
                device(y, core, x, zl_t, c_t),
            )
            if i == ZL - 1 and d == 0:
                @pl.when(other == 1)
                def _():
                    copy.start()

                @pl.when(other == 0)
                def _():
                    a_in[z] = a_out[zl * CORES + core]
            else:
                copy.start()
                a_copies.append(copy)
            last_copy = copy

    def landed(slot):
        remote(
            a_out.at[0], a_in.at[slot], a_send.at[0], a_recv.at[slot], right
        ).wait_recv()

    @pl.when(other == 1)
    def _():
        landed(z)

    for i in range(1, ZH * ZL):
        landed((z + i) % (ZH * ZL))
    piece = a_in[0]
    for i in range(1, ZH * ZL):
        piece = piece + a_in[i]

    for i in range(X):
        b_out[i] = piece[:, i * per:(i + 1) * per, :]
    b_copies = []
    for dx in (2, 1, 3) if X == 4 else range(1, X):
        x_t = (x + dx) % X
        copy = remote(
            b_out.at[x_t], b_in.at[x], b_send.at[x_t], b_recv.at[x],
            device(y, zh, x_t, zl, core),
        )
        copy.start()
        b_copies.append((copy, x_t))
    b_in[x] = b_out[x]
    for copy, x_t in b_copies:
        remote(b_out.at[0], b_in.at[x_t], b_send.at[x_t], b_recv.at[x_t], right).wait_recv()
    out[...] = b_in[...]

    for copy, _slot in factor + b_copies:
        copy.wait_send()
    for copy in (to_right, to_left, want_right, want_left):
        copy.wait_send()
    for side in range(2):
        for o in near:
            k_copy(side, o).wait_send()
    for copy in a_copies:
        copy.wait_send()

    @pl.when(other == 1)
    def _():
        last_copy.wait_send()


def on_device(density, momenta, desired, factor_x, factor_y, factor_m):
    members, rows, ny = density.shape
    ranks = factor_x.shape[1]
    ry = factor_y.shape[1]
    count = X * ZL * CORES
    per = ranks // count
    planes = X * CORES
    nk = Y * ZH * X
    f32 = jnp.float32
    vmem = pl.BlockSpec(memory_space=pltpu.VMEM)
    dma = pltpu.SemaphoreType.DMA
    strip = (rows + 2 * HALO, 3, members, ny)
    return pl.pallas_call(
        kernel,
        out_shape=jax.ShapeDtypeStruct((X, 3, per, ry), f32),
        in_specs=[pl.BlockSpec(memory_space=pltpu.HBM)] * 6,
        out_specs=vmem,
        scratch_shapes=[
            pltpu.VMEM((members, rows, ny), f32),
            pltpu.VMEM((members, 2, rows, ny), f32),
            pltpu.VMEM((2, 3 * rows, ny), f32),
            pltpu.VMEM((planes, rows, ranks), f32),
            pltpu.VMEM((ny, ry), f32),
            pltpu.VMEM((members, factor_m.shape[1]), f32),
            pltpu.VMEM(strip, f32),
            pltpu.VMEM(strip, f32),
            pltpu.VMEM(strip, f32),
            pltpu.VMEM(strip, f32),
            pltpu.VMEM((3, HALO, members, ny), f32),
            pltpu.VMEM((nk * rows, HALO * members), f32),
            pltpu.VMEM((ranks, planes * rows), f32),
            pltpu.VMEM((3, planes * rows, ry), f32),
            pltpu.VMEM((2, nk, 3, HALO, ry), f32),
            pltpu.VMEM((2, Y * planes, 3, HALO, ry), f32),
            pltpu.VMEM((ZL * CORES, 3, per * X, ry), f32),
            pltpu.VMEM((ZH * ZL, 3, per * X, ry), f32),
            pltpu.VMEM((X, 3, per, ry), f32),
            pltpu.VMEM((X, 3, per, ry), f32),
            dma((6,)), dma((2,)), dma((2,)), dma((2,)), dma((2,)),
            dma((planes,)), dma((planes,)),
            dma((2, Y * planes)), dma((2, Y * planes)),
            dma((ZL * CORES,)), dma((ZH * ZL,)),
            dma((X,)), dma((X,)),
        ],
        compiler_params=pltpu.CompilerParams(
            collective_id=0, has_side_effects=True, vmem_limit_bytes=67_043_328
        ),
    )(density, momenta, desired, factor_x, factor_y, factor_m)


def solution(mesh):
    return jax.shard_map(
        on_device,
        mesh=mesh,
        in_specs=(
            P("mem", "gx", None),
            P("mem", None, "gx", None),
            P(None, "gx", None),
            P("gx", None),
            P(),
            P("mem", None),
        ),
        out_specs=P("mem", None, "gx", None),
        check_vma=False,
    )
```

```python
import jax
import jax.numpy as jnp
from jax import lax
from jax.experimental import pallas as pl
from jax.experimental.pallas import tpu as pltpu
from jax.sharding import PartitionSpec as P

Y, ZH, X, ZL, CORES = 4, 2, 4, 8, 2
STEPS = 2
DTIME = 0.2
HALO = 4
PAIR = 2
TILE = 8
MESH = pl.DeviceIdType.MESH
HIGHEST = lax.Precision.HIGHEST


def primitive(q):
    rho, mx, my = q
    inverse = 1.0 / rho
    u = mx * inverse
    v = my * inverse
    sound = jnp.sqrt(rho)
    pressure = 0.5 * rho * rho
    cross = mx * v
    return dict(
        q=q,
        fx=(mx, mx * u + pressure, cross),
        gy=(my, cross, my * v + pressure),
        rx=jnp.abs(u) + sound,
        ry=jnp.abs(v) + sound,
    )


def faces_x(a, b):
    bound = jnp.maximum(a["rx"], b["rx"])
    return tuple(
        (fa + fb) - bound * (qb - qa)
        for fa, fb, qa, qb in zip(a["fx"], b["fx"], a["q"], b["q"])
    )


def ahead(t):
    return pltpu.roll(t, t.shape[-1] - 1, axis=t.ndim - 1)


def behind(t):
    return pltpu.roll(t, 1, axis=t.ndim - 1)


def slopes_y(a):
    bound = jnp.maximum(a["ry"], ahead(a["ry"]))
    q_next = tuple(ahead(t) for t in a["q"])
    g_next = (q_next[2], ahead(a["gy"][1]), ahead(a["gy"][2]))
    out = []
    for g, gn, q, qn in zip(a["gy"], g_next, a["q"], q_next):
        face = (g + gn) - bound * (qn - q)
        out.append(face - behind(face))
    return out


def sweep(source, store, desired_row, start, count, tile):
    def tile_step(index, carry):
        sub = pl.ds(pl.multiple_of(index * tile, tile), tile)

        def row(r):
            return primitive(tuple(source[r, c, sub, :] for c in range(3)))

        before, here = row(start - 1), row(start)
        face_before = faces_x(before, here)
        for i in range(count):
            r = start + i
            after = row(r + 1)
            face_after = faces_x(here, after)
            gy = slopes_y(here)
            new = []
            for c in range(3):
                flux = (face_after[c] - face_before[c]) + gy[c]
                value = here["q"][c] - (0.5 * DTIME) * flux
                if c:
                    wish = jnp.broadcast_to(desired_row(c - 1, r), value.shape)
                    value = value + DTIME * (here["q"][0] * wish - here["q"][c])
                new.append(value)
            store(i, r, sub, new)
            here, face_before = after, face_after
        return carry

    return tile_step


def halves(t):
    top = t.astype(jnp.bfloat16)
    return top, (t - top.astype(jnp.float32)).astype(jnp.bfloat16)


def mul(a, b):
    return jnp.dot(a, b, preferred_element_type=jnp.float32)


def exact(a, b):
    return lax.dot_general(
        a, b, (((1,), (1,)), ((), ())),
        precision=HIGHEST, preferred_element_type=jnp.float32,
    )


def index(shape, dim):
    return lax.broadcasted_iota(jnp.int32, shape, dim)


def one_hot(mask):
    return mask.astype(jnp.float32)


def interleave(low, high):
    width = low.shape[-1]
    first = index(low.shape, low.ndim - 1) < width // 2
    def turn(t):
        return pltpu.roll(t, width // 2, axis=t.ndim - 1)
    return jnp.where(first, low, turn(high)), jnp.where(first, turn(low), high)


def hops(offset, extent):
    return min(offset % extent, (-offset) % extent)


def kernel(
    dens_hbm, mom_hbm, want_hbm, fx_hbm, fy_hbm, fm_hbm, out,
    dens, mom, want, fx_all, fy, fm,
    strip0, strip1, strip2, strip3, final, fy2, weight, turned,
    k_out, k_in, a_out, a_in, b_out, b_in,
    in_sem, h_send, h_recv, d_send, d_recv, f_send, f_recv,
    k_send, k_recv, a_send, a_recv, b_send, b_recv,
):
    members, rows, ny = dens_hbm.shape
    tile = min(members, 8)
    ry = fy.shape[1]
    ranks = fx_all.shape[2]
    kb = X
    planes = PAIR * X * CORES
    nk = Y * ZH * kb
    nz = ZH * ZL
    f32 = jnp.float32
    mem, gx = lax.axis_index("mem"), lax.axis_index("gx")
    y, zh = lax.div(mem, ZH), lax.rem(mem, ZH)
    core = lax.rem(gx, CORES)
    zl = lax.rem(lax.div(gx, CORES), ZL)
    x = lax.div(gx, CORES * ZL)
    half = lax.rem(zl, PAIR)
    base = zl - half
    z = zh * ZL + zl
    other = lax.rem(zh + core, 2)

    def device(y_, zh_, x_, zl_, core_):
        return (y_ * ZH + zh_, (x_ * ZL + zl_) * CORES + core_)

    def source(q_, x_, c_):
        return (q_ * X + x_) * CORES + c_

    count = X * ZL * CORES
    per = ranks // count
    right = (mem, lax.rem(gx + 1, count))
    left = (mem, lax.rem(gx + count - 1, count))
    near = [
        (dy, dq, dx, dc)
        for dy in range(Y) for dq in range(PAIR) for dx in range(X) for dc in range(CORES)
        if dy or dq or dx or dc
    ]
    near.sort(key=lambda o: -(hops(o[0], Y) + o[1] + hops(o[2], X)))
    ys = [y] + [lax.rem(y + i, Y) for i in range(1, Y)]
    qs = [half] + [lax.rem(half + i, PAIR) for i in range(1, PAIR)]
    xs = [x] + [lax.rem(x + i, X) for i in range(1, X)]
    cs = [core] + [lax.rem(core + i, CORES) for i in range(1, CORES)]

    def group(o):
        return ys[o[0]], qs[o[1]], xs[o[2]], cs[o[3]]

    def group_device(o):
        y_, q_, x_, c_ = group(o)
        return device(y_, zh, x_, base + q_, c_)

    mine = y * planes + source(half, x, core)

    fetch = [
        pltpu.make_async_copy(src, dst, in_sem.at[i])
        for i, (src, dst) in enumerate([
            (dens_hbm, dens), (mom_hbm, mom), (want_hbm, want.at[:, pl.ds(rows, rows), :]),
            (fx_hbm, fx_all.at[source(half, x, core)]), (fy_hbm, fy), (fm_hbm, fm),
        ])
    ]
    for copy in fetch:
        copy.start()

    barrier = pltpu.get_barrier_semaphore()

    def greet(who):
        pl.semaphore_signal(barrier, inc=1, device_id=who, device_id_type=MESH)

    greet(right)
    greet(left)
    for i in sorted(range(1, nz), key=lambda i: -hops(i, nz)):
        zz = lax.rem(z + i, nz)
        greet(device(y, lax.div(zz, ZL), x, lax.rem(zz, ZL), zh))

    @pl.when(other == 1)
    def _():
        greet(device(y, zh, x, zl, zh))

    for o in near:
        greet(group_device(o))

    for copy in fetch[:2]:
        copy.wait()
    for r in range(rows):
        strip0[HALO + r, 0] = dens[:, r, :]
        strip0[HALO + r, 1] = mom[:, 0, r, :]
        strip0[HALO + r, 2] = mom[:, 1, r, :]

    pl.semaphore_wait(barrier, 2 + (nz - 1) + len(near) + other)

    def remote(src, dst, send, recv, who):
        return pltpu.make_async_remote_copy(
            src_ref=src, dst_ref=dst, send_sem=send, recv_sem=recv,
            device_id=who, device_id_type=MESH,
        )

    to_right = remote(
        strip0.at[pl.ds(rows, HALO)], strip0.at[pl.ds(0, HALO)],
        h_send.at[0], h_recv.at[0], right,
    )
    to_left = remote(
        strip0.at[pl.ds(HALO, HALO)], strip0.at[pl.ds(HALO + rows, HALO)],
        h_send.at[1], h_recv.at[1], left,
    )
    want_right = remote(
        want_hbm, want.at[:, pl.ds(0, rows), :], d_send.at[0], d_recv.at[0], right
    )
    want_left = remote(
        want_hbm, want.at[:, pl.ds(2 * rows, rows), :], d_send.at[1], d_recv.at[1], left
    )
    later_right = (core == 1) & (zl <= 2)
    later_left = (core == 0) & (zl >= ZL - 3)

    @pl.when(jnp.logical_not(later_right))
    def _():
        to_right.start()

    @pl.when(jnp.logical_not(later_left))
    def _():
        to_left.start()

    want_right.start()
    want_left.start()

    factor = []
    for o in near:
        if o[0] == 0:
            copy = remote(
                fx_hbm, fx_all.at[source(half, x, core)],
                f_send.at[source(*group(o)[1:])], f_recv.at[source(half, x, core)],
                group_device(o),
            )
            copy.start()
            factor.append((copy, source(*group(o)[1:])))
    for copy in fetch[2:]:
        copy.wait()

    def desired_row(c, r):
        return want[c, pl.ds(r + rows - HALO, 1), :]

    strips = (strip0, strip1, strip2, strip3)

    def section(e, start, n):
        def store(i, r, sub, new):
            for c in range(3):
                value = new[c]
                if e % 2:
                    value = 0.5 * strips[e - 1][r, c, sub, :] + 0.5 * value
                if e == 2 * STEPS - 1:
                    final[i // 2, c, i % 2, sub, :] = value
                else:
                    strips[e + 1][r, c, sub, :] = value

        lax.fori_loop(
            0, members // tile, sweep(strips[e], store, desired_row, start, n, tile), 0
        )

    for e in range(2 * STEPS - 1):
        section(e, HALO + 1 + e, rows - 2 - 2 * e)

    @pl.when(later_right)
    def _():
        to_right.start()

    @pl.when(later_left)
    def _():
        to_left.start()

    top, rest = halves(fy[...])
    fy2[:, :ry] = top
    fy2[:, ry:] = rest

    shape = (nk * TILE, 3 * 2 * members)
    tall = exact(one_hot(index((nk * TILE, nk), 0) // TILE == index((nk * TILE, nk), 1)), fm[...])
    spread = one_hot(index((shape[1], members), 0) % members == index((shape[1], members), 1))
    wide = exact(tall, spread)
    wide = jnp.where(index(shape, 0) % TILE == index(shape, 1) // members, wide, 0.0)
    top, rest = halves(wide)
    weight[0] = top
    weight[1] = rest

    for copy, them in factor:
        remote(fx_hbm, fx_all.at[them], f_send.at[them], f_recv.at[them], right).wait_recv()
    new = (per * ZL * CORES * 3 * X, ranks)
    line = index(new, 0)
    x_ = line % X
    c_ = (line // (X * 3)) % CORES
    zl_ = (line // (X * 3 * CORES)) % ZL
    t_ = line // (X * 3 * CORES * ZL)
    picked = exact(
        one_hot(index(new, 1) == ((x_ * ZL + zl_) * CORES + c_) * per + t_),
        fx_all[...].reshape(planes * rows, ranks),
    )
    wide = (2 * planes * TILE, planes * rows)
    at = index(wide, 0)
    side_, source_, row_ = at // (planes * TILE), (at // TILE) % planes, at % 2
    both = (new[0], wide[0])
    keep = (index(both, 0) // X) % 3 == (index(both, 1) % TILE) // 2
    for rh in range(2):
        place = one_hot(index(wide, 1) == source_ * rows + side_ * HALO + rh * 2 + row_)
        top, rest = halves(jnp.where(keep, exact(picked, place), 0.0))
        turned[rh, 0] = top
        turned[rh, 1] = rest

    def k_of(y_, x_, c_):
        return (y_ * ZH + c_) * kb + x_

    def k_copy(side, o):
        y_, q_, x_, c_ = group(o)
        slot = y_ * planes + source(q_, x_, c_)
        return remote(
            k_out.at[side, k_of(y_, x_, c_), q_], k_in.at[side, mine],
            k_send.at[side, slot], k_recv.at[side, mine], group_device(o),
        )

    def one_side(turn, carry):
        side = (1 - core) + turn * (2 * core - 1)
        remote(
            strip0.at[pl.ds(HALO, HALO)], strip0.at[pl.ds(side * (HALO + rows), HALO)],
            h_send.at[side], h_recv.at[side], right,
        ).wait_recv()
        remote(
            want_hbm, want.at[:, pl.ds(pl.multiple_of(side * 2 * rows, rows), rows), :],
            d_send.at[side], d_recv.at[side], right,
        ).wait_recv()
        for e in range(2 * STEPS):
            section(e, 1 + e + side * (rows + 2 - 2 * e), HALO)
        top, rest = halves(final[...].reshape(2 * 3 * 2 * members, ny))
        twice = mul(top, fy2[...])
        along_y = twice[:, :ry] + twice[:, ry:] + mul(rest, fy2[:, :ry])
        deep = 3 * 2 * members
        top, rest = halves(jnp.concatenate([along_y[:deep], along_y[deep:]], axis=1))
        terms = mul(weight[0], top) + mul(weight[0], rest) + mul(weight[1], top)
        parts = interleave(terms[:, :ry], terms[:, ry:])
        for q_ in range(PAIR):
            k_out[side, :, q_] = parts[q_].reshape(nk, TILE, ry)
        for o in near:
            k_copy(side, o).start()
        k_in[side, mine] = k_out[side, k_of(y, x, core), half]
        return carry

    lax.fori_loop(0, 2, one_side, 0)

    for side in range(2):
        for o in reversed(near):
            y_, q_, x_, c_ = group(o)
            slot = y_ * planes + source(q_, x_, c_)
            remote(
                k_out.at[0, 0, 0], k_in.at[side, slot],
                k_send.at[side, slot], k_recv.at[side, slot], right,
            ).wait_recv()
    total = k_in[:, pl.ds(0, planes)]
    for i in range(1, Y):
        total = total + k_in[:, pl.ds(i * planes, planes)]

    top, rest = halves(total.reshape(2 * planes * TILE, ry))
    cat = jnp.concatenate([top, rest], axis=1)

    def expand(rh):
        twice = mul(turned[rh, 0], cat)
        return twice[:, :ry] + twice[:, ry:] + mul(turned[rh, 1], top)

    even = expand(0)
    odd = expand(1)
    summed = even + pltpu.roll(odd, ry // 2, axis=1)
    mid = new[0] // per
    packed = interleave(summed[:mid], summed[mid:])[0]
    for i in range(ZL * CORES * 3):
        a_out[i // 3, i % 3] = packed[i * X:(i + 1) * X]

    a_copies = []
    far = sorted(range(ZL), key=lambda s: (hops(s, ZL) * -1, s))
    for i in range(ZL):
        s = far[i] + other * (far[ZL - 1 - i] - far[i])
        zl_t = lax.rem(zl + s, ZL)
        for d in (1, 0):
            c_t = cs[d]
            slot = zl_t * CORES + c_t
            copy = remote(
                a_out.at[slot], a_in.at[z], a_send.at[slot], a_recv.at[z],
                device(y, core, x, zl_t, c_t),
            )
            if i == ZL - 1 and d == 0:
                @pl.when(other == 1)
                def _():
                    copy.start()

                @pl.when(other == 0)
                def _():
                    a_in[z] = a_out[zl * CORES + core]
            else:
                copy.start()
                a_copies.append(copy)
            last_copy = copy

    def landed(slot):
        remote(
            a_out.at[0], a_in.at[slot], a_send.at[0], a_recv.at[slot], right
        ).wait_recv()

    @pl.when(other == 1)
    def _():
        landed(z)

    for i in range(1, nz):
        landed(lax.rem(z + i, nz))
    pieces = []
    for q_ in range(PAIR):
        piece = a_in[q_]
        for i in range(PAIR, nz, PAIR):
            piece = piece + a_in[i + q_]
        pieces.append(piece)
    pieces = interleave(*pieces)

    for i in range(X):
        for t in range(per):
            b_out[i, :, t] = pieces[t][:, i]
    b_copies = []
    for dx in (2, 1, 3):
        copy = remote(
            b_out.at[xs[dx]], b_in.at[x], b_send.at[xs[dx]], b_recv.at[x],
            device(y, zh, xs[dx], zl, core),
        )
        copy.start()
        b_copies.append((copy, xs[dx]))
    b_in[x] = b_out[x]
    for copy, x_t in b_copies:
        remote(b_out.at[0], b_in.at[x_t], b_send.at[x_t], b_recv.at[x_t], right).wait_recv()
    out[...] = b_in[...]

    for copy, _slot in factor + b_copies:
        copy.wait_send()
    for copy in (to_right, to_left, want_right, want_left):
        copy.wait_send()
    for side in range(2):
        for o in near:
            k_copy(side, o).wait_send()
    for copy in a_copies:
        copy.wait_send()

    @pl.when(other == 1)
    def _():
        last_copy.wait_send()


def on_device(density, momenta, desired, factor_x, factor_y, factor_m):
    members, rows, ny = density.shape
    ranks = factor_x.shape[1]
    ry = factor_y.shape[1]
    count = X * ZL * CORES
    per = ranks // count
    planes = PAIR * X * CORES
    nk = Y * ZH * X
    f32 = jnp.float32
    vmem = pl.BlockSpec(memory_space=pltpu.VMEM)
    dma = pltpu.SemaphoreType.DMA
    strip = (rows + 2 * HALO, 3, members, ny)
    return pl.pallas_call(
        kernel,
        out_shape=jax.ShapeDtypeStruct((X, 3, per, ry), f32),
        in_specs=[pl.BlockSpec(memory_space=pltpu.HBM)] * 6,
        out_specs=vmem,
        scratch_shapes=[
            pltpu.VMEM((members, rows, ny), f32),
            pltpu.VMEM((members, 2, rows, ny), f32),
            pltpu.VMEM((2, 3 * rows, ny), f32),
            pltpu.VMEM((planes, rows, ranks), f32),
            pltpu.VMEM((ny, ry), f32),
            pltpu.VMEM((members, factor_m.shape[1]), f32),
            pltpu.VMEM(strip, f32),
            pltpu.VMEM(strip, f32),
            pltpu.VMEM(strip, f32),
            pltpu.VMEM(strip, f32),
            pltpu.VMEM((2, 3, 2, members, ny), f32),
            pltpu.VMEM((ny, 2 * ry), jnp.bfloat16),
            pltpu.VMEM((2, nk * TILE, 3 * 2 * members), jnp.bfloat16),
            pltpu.VMEM((2, 2, per * ZL * CORES * 3 * X, 2 * planes * TILE), jnp.bfloat16),
            pltpu.VMEM((2, nk, PAIR, TILE, ry), f32),
            pltpu.VMEM((2, Y * planes, TILE, ry), f32),
            pltpu.VMEM((ZL * CORES, 3, X, ry), f32),
            pltpu.VMEM((ZH * ZL, 3, X, ry), f32),
            pltpu.VMEM((X, 3, per, ry), f32),
            pltpu.VMEM((X, 3, per, ry), f32),
            dma((6,)), dma((2,)), dma((2,)), dma((2,)), dma((2,)),
            dma((planes,)), dma((planes,)),
            dma((2, Y * planes)), dma((2, Y * planes)),
            dma((ZL * CORES,)), dma((ZH * ZL,)),
            dma((X,)), dma((X,)),
        ],
        compiler_params=pltpu.CompilerParams(
            collective_id=0, has_side_effects=True, vmem_limit_bytes=67_043_328
        ),
    )(density, momenta, desired, factor_x, factor_y, factor_m)


def solution(mesh):
    return jax.shard_map(
        on_device,
        mesh=mesh,
        in_specs=(
            P("mem", "gx", None),
            P("mem", None, "gx", None),
            P(None, "gx", None),
            P("gx", None),
            P(),
            P("mem", None),
        ),
        out_specs=P("mem", None, "gx", None),
        check_vma=False,
    )
```

```python
import jax
import jax.numpy as jnp
from jax import lax
from jax.experimental import pallas as pl
from jax.experimental.pallas import tpu as pltpu
from jax.sharding import PartitionSpec as P

Y, ZH, X, ZL, CORES = 4, 2, 4, 8, 2
STEPS = 2
DTIME = 0.2
HALO = 4
MESH = pl.DeviceIdType.MESH
HIGHEST = lax.Precision.HIGHEST


def primitive(q):
    rho, mx, my = q
    root = lax.rsqrt(rho)
    inverse = root * root
    u = mx * inverse
    v = my * inverse
    sound = rho * root
    pressure = 0.5 * rho * rho
    cross = mx * v
    return dict(
        q=q,
        fx=(mx, mx * u + pressure, cross),
        gy=(my, cross, my * v + pressure),
        rx=jnp.abs(u) + sound,
        ry=jnp.abs(v) + sound,
    )


def faces_x(a, b):
    bound = jnp.maximum(a["rx"], b["rx"])
    return tuple(
        (fa + fb) - bound * (qb - qa)
        for fa, fb, qa, qb in zip(a["fx"], b["fx"], a["q"], b["q"])
    )


def ahead(t):
    return pltpu.roll(t, t.shape[-1] - 1, axis=t.ndim - 1)


def behind(t):
    return pltpu.roll(t, 1, axis=t.ndim - 1)


def slopes_y(a):
    bound = jnp.maximum(a["ry"], ahead(a["ry"]))
    q_next = tuple(ahead(t) for t in a["q"])
    g_next = (q_next[2], ahead(a["gy"][1]), ahead(a["gy"][2]))
    out = []
    for g, gn, q, qn in zip(a["gy"], g_next, a["q"], q_next):
        face = (g + gn) - bound * (qn - q)
        out.append(face - behind(face))
    return out


def sweep(source, store, desired_row, start, count, tile):
    def tile_step(index, carry):
        sub = pl.ds(pl.multiple_of(index * tile, tile), tile)

        def row(r):
            return primitive(tuple(source[r, c, sub, :] for c in range(3)))

        before, here = row(start - 1), row(start)
        face_before = faces_x(before, here)
        for i in range(count):
            r = start + i
            after = row(r + 1)
            face_after = faces_x(here, after)
            gy = slopes_y(here)
            new = []
            for c in range(3):
                flux = (face_after[c] - face_before[c]) + gy[c]
                value = here["q"][c] - (0.5 * DTIME) * flux
                if c:
                    wish = jnp.broadcast_to(desired_row(c - 1, r), value.shape)
                    value = value + DTIME * (here["q"][0] * wish - here["q"][c])
                new.append(value)
            store(r, sub, new)
            here, face_before = after, face_after
        return carry

    return tile_step


def halves(t):
    top = t.astype(jnp.bfloat16)
    return top, (t - top.astype(jnp.float32)).astype(jnp.bfloat16)


def mul(a, b):
    return jnp.dot(a, b, preferred_element_type=jnp.float32)


def hops(offset, extent):
    return min(offset % extent, (-offset) % extent)


def kernel(
    dens_hbm, mom_hbm, want_hbm, fx_hbm, fy_hbm, fm_hbm, out,
    dens, mom, want, fx_all, fy, fm,
    strip0, strip1, strip2, strip3, final, fy2, weight, turned, gathered,
    k_out, k_in, a_out, a_in, b_out, b_in,
    rounds, in_sem, h_send, h_recv, d_send, d_recv, f_send, f_recv,
    k_send, k_recv, a_send, a_recv, b_send, b_recv,
):
    members, rows, ny = dens_hbm.shape
    tile = min(members, 8)
    ry = fy.shape[1]
    kb = X
    planes = X * CORES
    nk = Y * ZH * kb
    mem, gx = lax.axis_index("mem"), lax.axis_index("gx")
    y, zh = lax.div(mem, ZH), lax.rem(mem, ZH)
    core = lax.rem(gx, CORES)
    zl = lax.rem(lax.div(gx, CORES), ZL)
    x = lax.div(gx, CORES * ZL)
    xc = x * CORES + core
    z = zh * ZL + zl
    nz = ZH * ZL
    other = lax.rem(zh + core, 2)

    def device(y_, zh_, x_, zl_, core_):
        return (y_ * ZH + zh_, (x_ * ZL + zl_) * CORES + core_)

    count = X * ZL * CORES
    right = (mem, lax.rem(gx + 1, count))
    left = (mem, lax.rem(gx + count - 1, count))
    near = [
        (dy, dx, dc)
        for dy in range(Y) for dx in range(X) for dc in range(CORES)
        if dy or dx or dc
    ]
    near.sort(key=lambda o: -(hops(o[0], Y) + hops(o[1], X)))

    ys = [y] + [lax.rem(y + i, Y) for i in range(1, Y)]
    xs = [x] + [lax.rem(x + i, X) for i in range(1, X)]
    cs = [core] + [lax.rem(core + i, CORES) for i in range(1, CORES)]

    def in_plane(dy, dx, dc):
        return ys[dy], xs[dx], cs[dc]

    fetch = [
        pltpu.make_async_copy(src, dst, in_sem.at[i])
        for i, (src, dst) in enumerate([
            (dens_hbm, dens), (mom_hbm, mom), (want_hbm, want.at[:, pl.ds(rows, rows), :]),
            (fx_hbm, fx_all.at[xc]), (fy_hbm, fy), (fm_hbm, fm),
        ])
    ]
    for copy in fetch:
        copy.start()

    barrier = pltpu.get_barrier_semaphore()

    def tell(semaphore, who):
        pl.semaphore_signal(semaphore, inc=1, device_id=who, device_id_type=MESH)

    def along_z(i):
        zz = lax.rem(z + i, nz)
        return device(y, lax.div(zz, ZL), x, lax.rem(zz, ZL), core)

    mate = device(y, zh, x, zl, cs[1])
    y_peers = [device(ys[i], zh, x, zl, core) for i in range(1, Y)]
    x_peers = [device(y, zh, xs[i], zl, core) for i in range(1, X)]
    greeted = [right, left] + y_peers + x_peers + [along_z(1), along_z(nz - 1)]
    for who in greeted:
        tell(barrier, who)

    for copy in fetch[:2]:
        copy.wait()
    for r in range(rows):
        strip0[HALO + r, 0] = dens[:, r, :]
        strip0[HALO + r, 1] = mom[:, 0, r, :]
        strip0[HALO + r, 2] = mom[:, 1, r, :]

    pl.semaphore_wait(barrier, len(greeted))

    def remote(src, dst, send, recv, who):
        return pltpu.make_async_remote_copy(
            src_ref=src, dst_ref=dst, send_sem=send, recv_sem=recv,
            device_id=who, device_id_type=MESH,
        )

    to_right = remote(
        strip0.at[pl.ds(rows, HALO)], strip0.at[pl.ds(0, HALO)],
        h_send.at[0], h_recv.at[0], right,
    )
    to_left = remote(
        strip0.at[pl.ds(HALO, HALO)], strip0.at[pl.ds(HALO + rows, HALO)],
        h_send.at[1], h_recv.at[1], left,
    )
    want_right = remote(
        want_hbm, want.at[:, pl.ds(0, rows), :], d_send.at[0], d_recv.at[0], right
    )
    want_left = remote(
        want_hbm, want.at[:, pl.ds(2 * rows, rows), :], d_send.at[1], d_recv.at[1], left
    )
    later_right = (core == 1) & (zl <= 2)
    later_left = (core == 0) & (zl >= ZL - 3)

    @pl.when(jnp.logical_not(later_right))
    def _():
        to_right.start()

    @pl.when(jnp.logical_not(later_left))
    def _():
        to_left.start()

    want_right.start()
    want_left.start()
    second = x_peers + [along_z(1), along_z(nz - 1)]
    for who in second:
        tell(rounds.at[0], who)

    for copy in fetch[2:]:
        copy.wait()

    def desired_row(c, r):
        return want[c, pl.ds(r + rows - HALO, 1), :]

    strips = (strip0, strip1, strip2, strip3)

    def section(e, start, count, side=None):
        def store(r, sub, new):
            for c in range(3):
                value = new[c]
                if e % 2:
                    value = 0.5 * strips[e - 1][r, c, sub, :] + 0.5 * value
                if e == 2 * STEPS - 1:
                    final[c, r - start, sub, :] = value
                else:
                    strips[e + 1][r, c, sub, :] = value

        lax.fori_loop(
            0, members // tile, sweep(strips[e], store, desired_row, start, count, tile), 0
        )

    for e in range(2 * STEPS - 1):
        section(e, HALO + 1 + e, rows - 2 - 2 * e)

    pl.semaphore_wait(rounds.at[0], len(second))
    third = [mate, along_z(2), along_z(nz - 2)]
    for who in third:
        tell(rounds.at[1], who)

    @pl.when(later_right)
    def _():
        to_right.start()

    @pl.when(later_left)
    def _():
        to_left.start()

    shape = (nk * rows, HALO * members)
    pick = (
        lax.broadcasted_iota(jnp.int32, (nk * rows, nk), 0) // rows
        == lax.broadcasted_iota(jnp.int32, (nk * rows, nk), 1)
    ).astype(jnp.float32)
    spread = (
        lax.broadcasted_iota(jnp.int32, (members, HALO * members), 1) % members
        == lax.broadcasted_iota(jnp.int32, (members, HALO * members), 0)
    ).astype(jnp.float32)
    tall = lax.dot_general(
        pick, fm[...], (((1,), (1,)), ((), ())),
        precision=HIGHEST, preferred_element_type=jnp.float32,
    )
    wide = jnp.dot(tall, spread, precision=HIGHEST, preferred_element_type=jnp.float32)
    same_row = (
        lax.broadcasted_iota(jnp.int32, shape, 0) % rows
        == lax.broadcasted_iota(jnp.int32, shape, 1) // members
    )
    top, rest = halves(jnp.where(same_row, wide, 0.0))
    weight[0] = top
    weight[1] = rest
    top, rest = halves(fy[...])
    fy2[:, :ry] = top
    fy2[:, ry:] = rest

    pl.semaphore_wait(rounds.at[1], len(third))
    fourth = [along_z(4), along_z(nz - 4)]
    for who in fourth:
        tell(rounds.at[2], who)

    factor = []
    for o in near:
        if o[0] == 0:
            y_, x_, c_ = in_plane(*o)
            them = x_ * CORES + c_
            copy = remote(
                fx_hbm, fx_all.at[xc], f_send.at[them], f_recv.at[xc],
                device(y, zh, x_, zl, c_),
            )
            copy.start()
            factor.append((copy, them))
    for copy, them in factor:
        remote(fx_hbm, fx_all.at[them], f_send.at[them], f_recv.at[them], right).wait_recv()
    ranks = fx_all.shape[2]
    per = ranks // count
    new_a = lax.broadcasted_iota(jnp.int32, (ranks, ranks), 0)
    old_a = lax.broadcasted_iota(jnp.int32, (ranks, ranks), 1)
    t_ = new_a % per
    x_ = (new_a // per) % X
    c_ = (new_a // (per * X)) % CORES
    zl_ = new_a // (per * X * CORES)
    order = (old_a == ((x_ * ZL + zl_) * CORES + c_) * per + t_).astype(jnp.float32)
    top, rest = halves(lax.dot_general(
        order, fx_all[...].reshape(planes * rows, ranks), (((1,), (1,)), ((), ())),
        precision=HIGHEST, preferred_element_type=jnp.float32,
    ))
    turned[0] = top
    turned[1] = rest

    def k_of(y_, x_, c_):
        return (y_ * ZH + c_) * kb + x_

    mine = y * planes + xc

    def k_copy(side, o):
        y_, x_, c_ = in_plane(*o)
        slot = y_ * planes + x_ * CORES + c_
        return remote(
            k_out.at[side, k_of(y_, x_, c_)], k_in.at[side, mine],
            k_send.at[side, slot], k_recv.at[side, mine], device(y_, zh, x_, zl, c_),
        )

    def one_side(turn, carry):
        side = (1 - core) + turn * (2 * core - 1)
        remote(
            strip0.at[pl.ds(HALO, HALO)], strip0.at[pl.ds(side * (HALO + rows), HALO)],
            h_send.at[side], h_recv.at[side], right,
        ).wait_recv()
        remote(
            want_hbm, want.at[:, pl.ds(pl.multiple_of(side * 2 * rows, rows), rows), :],
            d_send.at[side], d_recv.at[side], right,
        ).wait_recv()
        for e in range(2 * STEPS):
            section(e, 1 + e + side * (rows + 2 - 2 * e), HALO)
        top, rest = halves(final[...].reshape(3 * HALO * members, ny))
        twice = mul(top, fy2[...])
        along_y = twice[:, :ry] + twice[:, ry:] + mul(rest, fy2[:, :ry])
        top, rest = halves(along_y.reshape(3, HALO * members, ry))
        for c in range(3):
            twice = mul(weight[0], jnp.concatenate([top[c], rest[c]], axis=1))
            terms = twice[:, :ry] + twice[:, ry:] + mul(weight[1], top[c])
            k_out[side, :, c] = terms.reshape(nk, rows, ry)[:, :HALO]
        for o in near:
            k_copy(side, o).start()
        k_in[side, mine] = k_out[side, k_of(y, x, core)]
        return carry

    lax.fori_loop(0, 2, one_side, 0)

    pl.semaphore_wait(rounds.at[2], len(fourth))
    tell(rounds.at[3], mate)

    for side in range(2):
        for o in reversed(near):
            y_, x_, c_ = in_plane(*o)
            slot = y_ * planes + x_ * CORES + c_
            remote(
                k_out.at[0, 0], k_in.at[side, slot],
                k_send.at[side, slot], k_recv.at[side, slot], right,
            ).wait_recv()
    for side in range(2):
        total = k_in[side, pl.ds(0, planes)]
        for i in range(1, Y):
            total = total + k_in[side, pl.ds(i * planes, planes)]
        for c in range(3):
            for i in range(planes):
                gathered[c, pl.ds(i * rows + side * HALO, HALO), :] = total[i, c]

    for c in range(3):
        top, rest = halves(gathered[c])
        twice = mul(turned[0], jnp.concatenate([top, rest], axis=1))
        a_out[:, c] = (
            twice[:, :ry] + twice[:, ry:] + mul(turned[1], top)
        ).reshape(ZL * CORES, per * X, ry)

    pl.semaphore_wait(rounds.at[3], 1)
    a_copies = []
    far = sorted(range(ZL), key=lambda s: (hops(s, ZL) * -1, s))
    for i in range(ZL):
        s = far[i] + other * (far[ZL - 1 - i] - far[i])
        zl_t = lax.rem(zl + s, ZL)
        for d in (1, 0):
            c_t = cs[d]
            slot = zl_t * CORES + c_t
            copy = remote(
                a_out.at[slot], a_in.at[z], a_send.at[slot], a_recv.at[z],
                device(y, core, x, zl_t, c_t),
            )
            if i == ZL - 1 and d == 0:
                @pl.when(other == 1)
                def _():
                    copy.start()

                @pl.when(other == 0)
                def _():
                    a_in[z] = a_out[zl * CORES + core]
            else:
                copy.start()
                a_copies.append(copy)
            last_copy = copy

    def landed(slot):
        remote(
            a_out.at[0], a_in.at[slot], a_send.at[0], a_recv.at[slot], right
        ).wait_recv()

    @pl.when(other == 1)
    def _():
        landed(z)

    for i in range(1, ZH * ZL):
        landed(lax.rem(z + i, nz))
    piece = a_in[0]
    for i in range(1, ZH * ZL):
        piece = piece + a_in[i]

    for i in range(X):
        b_out[i] = piece[:, i * per:(i + 1) * per, :]
    b_copies = []
    for dx in (2, 1, 3) if X == 4 else range(1, X):
        x_t = xs[dx]
        copy = remote(
            b_out.at[x_t], b_in.at[x], b_send.at[x_t], b_recv.at[x],
            device(y, zh, x_t, zl, core),
        )
        copy.start()
        b_copies.append((copy, x_t))
    b_in[x] = b_out[x]
    for copy, x_t in b_copies:
        remote(b_out.at[0], b_in.at[x_t], b_send.at[x_t], b_recv.at[x_t], right).wait_recv()
    out[...] = b_in[...]

    for copy, _slot in factor + b_copies:
        copy.wait_send()
    for copy in (to_right, to_left, want_right, want_left):
        copy.wait_send()
    for side in range(2):
        for o in near:
            k_copy(side, o).wait_send()
    for copy in a_copies:
        copy.wait_send()

    @pl.when(other == 1)
    def _():
        last_copy.wait_send()


def on_device(density, momenta, desired, factor_x, factor_y, factor_m):
    members, rows, ny = density.shape
    ranks = factor_x.shape[1]
    ry = factor_y.shape[1]
    count = X * ZL * CORES
    per = ranks // count
    planes = X * CORES
    nk = Y * ZH * X
    f32 = jnp.float32
    vmem = pl.BlockSpec(memory_space=pltpu.VMEM)
    dma = pltpu.SemaphoreType.DMA
    strip = (rows + 2 * HALO, 3, members, ny)
    return pl.pallas_call(
        kernel,
        out_shape=jax.ShapeDtypeStruct((X, 3, per, ry), f32),
        in_specs=[pl.BlockSpec(memory_space=pltpu.HBM)] * 6,
        out_specs=vmem,
        scratch_shapes=[
            pltpu.VMEM((members, rows, ny), f32),
            pltpu.VMEM((members, 2, rows, ny), f32),
            pltpu.VMEM((2, 3 * rows, ny), f32),
            pltpu.VMEM((planes, rows, ranks), f32),
            pltpu.VMEM((ny, ry), f32),
            pltpu.VMEM((members, factor_m.shape[1]), f32),
            pltpu.VMEM(strip, f32),
            pltpu.VMEM(strip, f32),
            pltpu.VMEM(strip, f32),
            pltpu.VMEM(strip, f32),
            pltpu.VMEM((3, HALO, members, ny), f32),
            pltpu.VMEM((ny, 2 * ry), jnp.bfloat16),
            pltpu.VMEM((2, nk * rows, HALO * members), jnp.bfloat16),
            pltpu.VMEM((2, ranks, planes * rows), jnp.bfloat16),
            pltpu.VMEM((3, planes * rows, ry), f32),
            pltpu.VMEM((2, nk, 3, HALO, ry), f32),
            pltpu.VMEM((2, Y * planes, 3, HALO, ry), f32),
            pltpu.VMEM((ZL * CORES, 3, per * X, ry), f32),
            pltpu.VMEM((ZH * ZL, 3, per * X, ry), f32),
            pltpu.VMEM((X, 3, per, ry), f32),
            pltpu.VMEM((X, 3, per, ry), f32),
            pltpu.SemaphoreType.REGULAR((4,)), dma((6,)), dma((2,)), dma((2,)), dma((2,)), dma((2,)),
            dma((planes,)), dma((planes,)),
            dma((2, Y * planes)), dma((2, Y * planes)),
            dma((ZL * CORES,)), dma((ZH * ZL,)),
            dma((X,)), dma((X,)),
        ],
        compiler_params=pltpu.CompilerParams(
            collective_id=0, has_side_effects=True, vmem_limit_bytes=67_043_328
        ),
    )(density, momenta, desired, factor_x, factor_y, factor_m)


def solution(mesh):
    return jax.shard_map(
        on_device,
        mesh=mesh,
        in_specs=(
            P("mem", "gx", None),
            P("mem", None, "gx", None),
            P(None, "gx", None),
            P("gx", None),
            P(),
            P("mem", None),
        ),
        out_specs=P("mem", None, "gx", None),
        check_vma=False,
    )
```

```python
import jax
import jax.numpy as jnp
from jax import lax
from jax.experimental import pallas as pl
from jax.experimental.pallas import tpu as pltpu
from jax.sharding import PartitionSpec as P

Y, ZH, X, ZL, CORES = 4, 2, 4, 8, 2
STEPS = 2
DTIME = 0.2
HALO = 4
MESH = pl.DeviceIdType.MESH
HIGHEST = lax.Precision.HIGHEST


def primitive(q):
    rho, mx, my = q
    root = lax.rsqrt(rho)
    inverse = root * root
    u = mx * inverse
    v = my * inverse
    sound = rho * root
    pressure = 0.5 * rho * rho
    cross = mx * v
    return dict(
        q=q,
        fx=(mx, mx * u + pressure, cross),
        gy=(my, cross, my * v + pressure),
        rx=jnp.abs(u) + sound,
        ry=jnp.abs(v) + sound,
    )


def faces_x(a, b):
    bound = jnp.maximum(a["rx"], b["rx"])
    return tuple(
        (fa + fb) - bound * (qb - qa)
        for fa, fb, qa, qb in zip(a["fx"], b["fx"], a["q"], b["q"])
    )


def ahead(t):
    return pltpu.roll(t, t.shape[-1] - 1, axis=t.ndim - 1)


def behind(t):
    return pltpu.roll(t, 1, axis=t.ndim - 1)


def slopes_y(a):
    bound = jnp.maximum(a["ry"], ahead(a["ry"]))
    q_next = tuple(ahead(t) for t in a["q"])
    g_next = (q_next[2], ahead(a["gy"][1]), ahead(a["gy"][2]))
    out = []
    for g, gn, q, qn in zip(a["gy"], g_next, a["q"], q_next):
        face = (g + gn) - bound * (qn - q)
        out.append(face - behind(face))
    return out


def sweep(source, store, desired_row, start, count, tile):
    def tile_step(index, carry):
        sub = pl.ds(pl.multiple_of(index * tile, tile), tile)

        def row(r):
            return primitive(tuple(source[r, c, sub, :] for c in range(3)))

        before, here = row(start - 1), row(start)
        face_before = faces_x(before, here)
        for i in range(count):
            r = start + i
            after = row(r + 1)
            face_after = faces_x(here, after)
            gy = slopes_y(here)
            new = []
            for c in range(3):
                flux = (face_after[c] - face_before[c]) + gy[c]
                value = here["q"][c] - (0.5 * DTIME) * flux
                if c:
                    wish = jnp.broadcast_to(desired_row(c - 1, r), value.shape)
                    value = value + DTIME * (here["q"][0] * wish - here["q"][c])
                new.append(value)
            store(r, sub, new)
            here, face_before = after, face_after
        return carry

    return tile_step


def halves(t):
    top = t.astype(jnp.bfloat16)
    return top, (t - top.astype(jnp.float32)).astype(jnp.bfloat16)


def mul(a, b):
    return jnp.dot(a, b, preferred_element_type=jnp.float32)


def hops(offset, extent):
    return min(offset % extent, (-offset) % extent)


def kernel(
    dens_hbm, mom_hbm, want_hbm, fx_hbm, fy_hbm, fm_hbm, out,
    dens, mom, want, fx_all, fy, fm,
    strip0, strip1, strip2, strip3, final, fy2, weight, turned, gathered,
    k_out, k_in, a_out, a_in, b_out, b_in,
    rounds, in_sem, h_send, h_recv, d_send, d_recv, f_send, f_recv,
    k_send, k_recv, a_send, a_recv, b_send, b_recv,
):
    members, rows, ny = dens_hbm.shape
    tile = min(members, 8)
    ry = fy.shape[1]
    kb = X
    planes = X * CORES
    nk = Y * ZH * kb
    mem, gx = lax.axis_index("mem"), lax.axis_index("gx")
    y, zh = lax.div(mem, ZH), lax.rem(mem, ZH)
    core = lax.rem(gx, CORES)
    zl = lax.rem(lax.div(gx, CORES), ZL)
    x = lax.div(gx, CORES * ZL)
    xc = x * CORES + core
    z = zh * ZL + zl
    nz = ZH * ZL
    other = lax.rem(zh + core, 2)

    def device(y_, zh_, x_, zl_, core_):
        return (y_ * ZH + zh_, (x_ * ZL + zl_) * CORES + core_)

    count = X * ZL * CORES
    right = (mem, lax.rem(gx + 1, count))
    left = (mem, lax.rem(gx + count - 1, count))
    near = [
        (dy, dx, dc)
        for dy in range(Y) for dx in range(X) for dc in range(CORES)
        if dy or dx or dc
    ]
    near.sort(key=lambda o: -(hops(o[0], Y) + hops(o[1], X)))

    ys = [y] + [lax.rem(y + i, Y) for i in range(1, Y)]
    xs = [x] + [lax.rem(x + i, X) for i in range(1, X)]
    cs = [core] + [lax.rem(core + i, CORES) for i in range(1, CORES)]

    def in_plane(dy, dx, dc):
        return ys[dy], xs[dx], cs[dc]

    fetch = [
        pltpu.make_async_copy(src, dst, in_sem.at[i])
        for i, (src, dst) in enumerate([
            (dens_hbm, dens), (mom_hbm, mom), (want_hbm, want.at[:, pl.ds(rows, rows), :]),
            (fx_hbm, fx_all.at[xc]), (fy_hbm, fy), (fm_hbm, fm),
        ])
    ]
    for copy in fetch:
        copy.start()

    barrier = pltpu.get_barrier_semaphore()

    def tell(semaphore, who):
        pl.semaphore_signal(semaphore, inc=1, device_id=who, device_id_type=MESH)

    def along_z(i):
        zz = lax.rem(z + i, nz)
        return device(y, lax.div(zz, ZL), x, lax.rem(zz, ZL), core)

    mate = device(y, zh, x, zl, cs[1])
    y_peers = [device(ys[i], zh, x, zl, core) for i in range(1, Y)]
    x_peers = [device(y, zh, xs[i], zl, core) for i in range(1, X)]
    greeted = [right, left] + y_peers + x_peers + [along_z(1), along_z(nz - 1)]
    for who in greeted:
        tell(barrier, who)

    for copy in fetch[:2]:
        copy.wait()
    for r in range(rows):
        strip0[HALO + r, 0] = dens[:, r, :]
        strip0[HALO + r, 1] = mom[:, 0, r, :]
        strip0[HALO + r, 2] = mom[:, 1, r, :]

    pl.semaphore_wait(barrier, len(greeted))

    def remote(src, dst, send, recv, who):
        return pltpu.make_async_remote_copy(
            src_ref=src, dst_ref=dst, send_sem=send, recv_sem=recv,
            device_id=who, device_id_type=MESH,
        )

    to_right = remote(
        strip0.at[pl.ds(rows, HALO)], strip0.at[pl.ds(0, HALO)],
        h_send.at[0], h_recv.at[0], right,
    )
    to_left = remote(
        strip0.at[pl.ds(HALO, HALO)], strip0.at[pl.ds(HALO + rows, HALO)],
        h_send.at[1], h_recv.at[1], left,
    )
    want_right = remote(
        want_hbm, want.at[:, pl.ds(0, rows), :], d_send.at[0], d_recv.at[0], right
    )
    want_left = remote(
        want_hbm, want.at[:, pl.ds(2 * rows, rows), :], d_send.at[1], d_recv.at[1], left
    )
    later_right = (core == 1) & (zl <= 2)
    later_left = (core == 0) & (zl >= ZL - 3)

    @pl.when(jnp.logical_not(later_right))
    def _():
        to_right.start()

    @pl.when(jnp.logical_not(later_left))
    def _():
        to_left.start()

    want_right.start()
    want_left.start()
    second = x_peers + [along_z(1), along_z(nz - 1)]
    for who in second:
        tell(rounds.at[0], who)

    for copy in fetch[2:]:
        copy.wait()

    def desired_row(c, r):
        return want[c, pl.ds(r + rows - HALO, 1), :]

    strips = (strip0, strip1, strip2, strip3)

    def section(e, start, count, side=None):
        def store(r, sub, new):
            for c in range(3):
                value = new[c]
                if e % 2:
                    value = 0.5 * strips[e - 1][r, c, sub, :] + 0.5 * value
                if e == 2 * STEPS - 1:
                    final[c, r - start, sub, :] = value
                else:
                    strips[e + 1][r, c, sub, :] = value

        lax.fori_loop(
            0, members // tile, sweep(strips[e], store, desired_row, start, count, tile), 0
        )

    for e in range(2 * STEPS - 1):
        section(e, HALO + 1 + e, rows - 2 - 2 * e)

    @pl.when(later_right)
    def _():
        to_right.start()

    @pl.when(later_left)
    def _():
        to_left.start()

    shape = (nk * rows, HALO * members)
    pick = (
        lax.broadcasted_iota(jnp.int32, (nk * rows, nk), 0) // rows
        == lax.broadcasted_iota(jnp.int32, (nk * rows, nk), 1)
    ).astype(jnp.float32)
    spread = (
        lax.broadcasted_iota(jnp.int32, (members, HALO * members), 1) % members
        == lax.broadcasted_iota(jnp.int32, (members, HALO * members), 0)
    ).astype(jnp.float32)
    tall = lax.dot_general(
        pick, fm[...], (((1,), (1,)), ((), ())),
        precision=HIGHEST, preferred_element_type=jnp.float32,
    )
    wide = jnp.dot(tall, spread, precision=HIGHEST, preferred_element_type=jnp.float32)
    same_row = (
        lax.broadcasted_iota(jnp.int32, shape, 0) % rows
        == lax.broadcasted_iota(jnp.int32, shape, 1) // members
    )
    top, rest = halves(jnp.where(same_row, wide, 0.0))
    weight[0] = top
    weight[1] = rest
    top, rest = halves(fy[...])
    fy2[:, :ry] = top
    fy2[:, ry:] = rest

    pl.semaphore_wait(rounds.at[0], len(second))
    third = [mate, along_z(2), along_z(nz - 2)]
    for who in third:
        tell(rounds.at[1], who)

    factor = [
        (
            remote(
                fx_hbm, fx_all.at[xc], f_send.at[xs[dx] * CORES + cs[dc]], f_recv.at[xc],
                device(y, zh, xs[dx], zl, cs[dc]),
            ),
            xs[dx] * CORES + cs[dc],
        )
        for dy, dx, dc in near if dy == 0
    ]
    fourth = [along_z(4), along_z(nz - 4)]

    def k_of(y_, x_, c_):
        return (y_ * ZH + c_) * kb + x_

    mine = y * planes + xc

    def k_copy(side, o):
        y_, x_, c_ = in_plane(*o)
        slot = y_ * planes + x_ * CORES + c_
        return remote(
            k_out.at[side, k_of(y_, x_, c_)], k_in.at[side, mine],
            k_send.at[side, slot], k_recv.at[side, mine], device(y_, zh, x_, zl, c_),
        )

    def one_side(turn, carry):
        side = (1 - core) + turn * (2 * core - 1)
        remote(
            strip0.at[pl.ds(HALO, HALO)], strip0.at[pl.ds(side * (HALO + rows), HALO)],
            h_send.at[side], h_recv.at[side], right,
        ).wait_recv()
        remote(
            want_hbm, want.at[:, pl.ds(pl.multiple_of(side * 2 * rows, rows), rows), :],
            d_send.at[side], d_recv.at[side], right,
        ).wait_recv()
        for e in range(2 * STEPS):
            section(e, 1 + e + side * (rows + 2 - 2 * e), HALO)
        top, rest = halves(final[...].reshape(3 * HALO * members, ny))
        twice = mul(top, fy2[...])
        along_y = twice[:, :ry] + twice[:, ry:] + mul(rest, fy2[:, :ry])
        top, rest = halves(along_y.reshape(3, HALO * members, ry))
        for c in range(3):
            twice = mul(weight[0], jnp.concatenate([top[c], rest[c]], axis=1))
            terms = twice[:, :ry] + twice[:, ry:] + mul(weight[1], top[c])
            k_out[side, :, c] = terms.reshape(nk, rows, ry)[:, :HALO]

        @pl.when(turn == 0)
        def _():
            pl.semaphore_wait(rounds.at[1], len(third))
            for who in fourth:
                tell(rounds.at[2], who)

        for o in near:
            k_copy(side, o).start()

        @pl.when(turn == 0)
        def _():
            for copy, _slot in factor:
                copy.start()

        k_in[side, mine] = k_out[side, k_of(y, x, core)]
        return carry

    lax.fori_loop(0, 2, one_side, 0)

    pl.semaphore_wait(rounds.at[2], len(fourth))
    tell(rounds.at[3], mate)

    for copy, them in factor:
        remote(fx_hbm, fx_all.at[them], f_send.at[them], f_recv.at[them], right).wait_recv()
    ranks = fx_all.shape[2]
    per = ranks // count
    new_a = lax.broadcasted_iota(jnp.int32, (ranks, ranks), 0)
    old_a = lax.broadcasted_iota(jnp.int32, (ranks, ranks), 1)
    t_ = new_a % per
    x_ = (new_a // per) % X
    c_ = (new_a // (per * X)) % CORES
    zl_ = new_a // (per * X * CORES)
    order = (old_a == ((x_ * ZL + zl_) * CORES + c_) * per + t_).astype(jnp.float32)
    top, rest = halves(lax.dot_general(
        order, fx_all[...].reshape(planes * rows, ranks), (((1,), (1,)), ((), ())),
        precision=HIGHEST, preferred_element_type=jnp.float32,
    ))
    turned[0] = top
    turned[1] = rest


    for side in range(2):
        for o in reversed(near):
            y_, x_, c_ = in_plane(*o)
            slot = y_ * planes + x_ * CORES + c_
            remote(
                k_out.at[0, 0], k_in.at[side, slot],
                k_send.at[side, slot], k_recv.at[side, slot], right,
            ).wait_recv()
    for side in range(2):
        total = k_in[side, pl.ds(0, planes)]
        for i in range(1, Y):
            total = total + k_in[side, pl.ds(i * planes, planes)]
        for c in range(3):
            for i in range(planes):
                gathered[c, pl.ds(i * rows + side * HALO, HALO), :] = total[i, c]

    for c in range(3):
        top, rest = halves(gathered[c])
        twice = mul(turned[0], jnp.concatenate([top, rest], axis=1))
        a_out[:, c] = (
            twice[:, :ry] + twice[:, ry:] + mul(turned[1], top)
        ).reshape(ZL * CORES, per * X, ry)

    pl.semaphore_wait(rounds.at[3], 1)
    a_copies = []
    far = sorted(range(ZL), key=lambda s: (hops(s, ZL) * -1, s))
    for i in range(ZL):
        s = far[i] + other * (far[ZL - 1 - i] - far[i])
        zl_t = lax.rem(zl + s, ZL)
        for d in (1, 0):
            c_t = cs[d]
            slot = zl_t * CORES + c_t
            copy = remote(
                a_out.at[slot], a_in.at[z], a_send.at[slot], a_recv.at[z],
                device(y, core, x, zl_t, c_t),
            )
            if i == ZL - 1 and d == 0:
                @pl.when(other == 1)
                def _():
                    copy.start()

                @pl.when(other == 0)
                def _():
                    a_in[z] = a_out[zl * CORES + core]
            else:
                copy.start()
                a_copies.append(copy)
            last_copy = copy

    def landed(slot):
        remote(
            a_out.at[0], a_in.at[slot], a_send.at[0], a_recv.at[slot], right
        ).wait_recv()

    @pl.when(other == 1)
    def _():
        landed(z)

    for i in range(1, ZH * ZL):
        landed(lax.rem(z + i, nz))
    piece = a_in[0]
    for i in range(1, ZH * ZL):
        piece = piece + a_in[i]

    for i in range(X):
        b_out[i] = piece[:, i * per:(i + 1) * per, :]
    b_copies = []
    for dx in (2, 1, 3) if X == 4 else range(1, X):
        x_t = xs[dx]
        copy = remote(
            b_out.at[x_t], b_in.at[x], b_send.at[x_t], b_recv.at[x],
            device(y, zh, x_t, zl, core),
        )
        copy.start()
        b_copies.append((copy, x_t))
    b_in[x] = b_out[x]
    for copy, x_t in b_copies:
        remote(b_out.at[0], b_in.at[x_t], b_send.at[x_t], b_recv.at[x_t], right).wait_recv()
    out[...] = b_in[...]

    for copy, _slot in factor + b_copies:
        copy.wait_send()
    for copy in (to_right, to_left, want_right, want_left):
        copy.wait_send()
    for side in range(2):
        for o in near:
            k_copy(side, o).wait_send()
    for copy in a_copies:
        copy.wait_send()

    @pl.when(other == 1)
    def _():
        last_copy.wait_send()


def on_device(density, momenta, desired, factor_x, factor_y, factor_m):
    members, rows, ny = density.shape
    ranks = factor_x.shape[1]
    ry = factor_y.shape[1]
    count = X * ZL * CORES
    per = ranks // count
    planes = X * CORES
    nk = Y * ZH * X
    f32 = jnp.float32
    vmem = pl.BlockSpec(memory_space=pltpu.VMEM)
    dma = pltpu.SemaphoreType.DMA
    strip = (rows + 2 * HALO, 3, members, ny)
    return pl.pallas_call(
        kernel,
        out_shape=jax.ShapeDtypeStruct((X, 3, per, ry), f32),
        in_specs=[pl.BlockSpec(memory_space=pltpu.HBM)] * 6,
        out_specs=vmem,
        scratch_shapes=[
            pltpu.VMEM((members, rows, ny), f32),
            pltpu.VMEM((members, 2, rows, ny), f32),
            pltpu.VMEM((2, 3 * rows, ny), f32),
            pltpu.VMEM((planes, rows, ranks), f32),
            pltpu.VMEM((ny, ry), f32),
            pltpu.VMEM((members, factor_m.shape[1]), f32),
            pltpu.VMEM(strip, f32),
            pltpu.VMEM(strip, f32),
            pltpu.VMEM(strip, f32),
            pltpu.VMEM(strip, f32),
            pltpu.VMEM((3, HALO, members, ny), f32),
            pltpu.VMEM((ny, 2 * ry), jnp.bfloat16),
            pltpu.VMEM((2, nk * rows, HALO * members), jnp.bfloat16),
            pltpu.VMEM((2, ranks, planes * rows), jnp.bfloat16),
            pltpu.VMEM((3, planes * rows, ry), f32),
            pltpu.VMEM((2, nk, 3, HALO, ry), f32),
            pltpu.VMEM((2, Y * planes, 3, HALO, ry), f32),
            pltpu.VMEM((ZL * CORES, 3, per * X, ry), f32),
            pltpu.VMEM((ZH * ZL, 3, per * X, ry), f32),
            pltpu.VMEM((X, 3, per, ry), f32),
            pltpu.VMEM((X, 3, per, ry), f32),
            pltpu.SemaphoreType.REGULAR((4,)), dma((6,)), dma((2,)), dma((2,)), dma((2,)), dma((2,)),
            dma((planes,)), dma((planes,)),
            dma((2, Y * planes)), dma((2, Y * planes)),
            dma((ZL * CORES,)), dma((ZH * ZL,)),
            dma((X,)), dma((X,)),
        ],
        compiler_params=pltpu.CompilerParams(
            collective_id=0, has_side_effects=True, vmem_limit_bytes=67_043_328
        ),
    )(density, momenta, desired, factor_x, factor_y, factor_m)


def solution(mesh):
    return jax.shard_map(
        on_device,
        mesh=mesh,
        in_specs=(
            P("mem", "gx", None),
            P("mem", None, "gx", None),
            P(None, "gx", None),
            P("gx", None),
            P(),
            P("mem", None),
        ),
        out_specs=P("mem", None, "gx", None),
        check_vma=False,
    )
```
